256 devices in a mesh: grp: 32 (over y, z), head: 8 (over x, core).
Axes of the slice: x: 4, y: 4, z: 8, core: 2. Of those that a mesh axis runs over, the one named last changes fastest.
Arguments:
- tokens: bfloat16 [16384, 1024], P(('grp', 'head')), may hold values from -6 to 6
- norm_gain: float32 [1024], replicated, may hold values from 0.5 to 1.5
- w_qkv: bfloat16 [1024, 3072], replicated, may hold values from -0.1875 to 0.1875
- w_gates: bfloat16 [1024, 16], replicated, may hold values from -0.1875 to 0.1875
- conv_weight: float32 [4, 3072], replicated, may hold values from -3 to 3
- conv_state: bfloat16 [32, 3, 3072], P('grp'), may hold values from -6 to 6
- decay_rate: float32 [8], replicated, may hold values from 0.0005 to 0.1
- ridge: float32 [8], P('head'), may hold values from 0.25 to 2
- w_out: bfloat16 [1024, 1024], replicated, may hold values from -0.1875 to 0.1875
- cache_keys: bfloat16 [2048, 128, 8, 128], P('grp', None, 'head'), may hold values from -0.59765625 to 0.59765625
- cache_values: bfloat16 [2048, 128, 8, 128], P('grp', None, 'head'), may hold values from -6 to 6
- page_table: int32 [32, 64], replicated, may hold values from 0 to 2047, as said below
- cache_lengths: int32 [32], replicated, may hold values from 1 to 8192, 131072 in all
- group_prompt: int32 [32], replicated, may hold values from 0 to 31
- prompt_state: float32 [32, 8, 2, 128, 128], P('grp', 'head'), may hold values from -8 to 16
Outputs:
- layer_out: bfloat16 [16384, 1024], P(('grp', 'head'))
The draws below stay inside these ranges and needn't reach their ends.
Inputs may be any that keep to these rules, and one draw needn't show every extreme that they name: `page_table`: every pool page is named exactly once in the table; each pool shard of 64 consecutive pages holds exactly 2 pages of every group's requests. `cache_lengths`: some request has exactly 8192 cached tokens.
All inputs are finite; a program needn't handle non-finite values.
Results may differ from the reference program's by a relative error of at most 0.0045.
Values may be sent and summed in bfloat16 or wider, within the bound.
A program may use at most 128 MiB of HBM per device.

```python
import math
import jax
import jax.numpy as jnp
import numpy as np
from jax import lax

D = 1024
HEADS = 8
HDIM = 128
CONV = 4
NEW = 512
CG_STEPS = 8
PAGE = 128
REQ_GRP = 1
PAGES_MAX = 64
GROUPS = 32
PROMPTS = 32
REQS = 32
TOKENS = 16384
POOL = 2048


def draw_page_table(key, part):
    shard_pages = REQ_GRP * PAGES_MAX
    per_group = shard_pages // GROUPS
    key_place, key_local = jax.random.split(key)
    place_keys = jax.random.split(key_place, GROUPS)
    placed = jax.vmap(lambda k: jax.random.permutation(k, shard_pages))(place_keys)
    local_keys = jax.random.split(key_local, GROUPS)
    local_perm = jax.vmap(lambda k: jax.random.permutation(k, shard_pages))(local_keys)
    shard_of = placed // per_group
    group_ids = jnp.arange(GROUPS)[:, None]
    before_perm = group_ids * per_group + placed % per_group
    page_ids = shard_of * shard_pages + local_perm[shard_of, before_perm]
    return page_ids.reshape(REQS, PAGES_MAX).astype(jnp.int32)


def draw_group_prompt(key, part):
    key_pick, key_far = jax.random.split(jax.random.fold_in(key, 71))
    picks = jax.random.randint(key_pick, (GROUPS,), 0, PROMPTS)
    far_group = jax.random.randint(key_far, (), 0, GROUPS)
    group_ids = jnp.arange(GROUPS)
    far_prompt = (group_ids + GROUPS // 2) % PROMPTS
    return jnp.where(group_ids == far_group, far_prompt, picks).astype(jnp.int32)


def draw_prompt_state(key, part):
    key_diag, key_off, key_cross = jax.random.split(key, 3)
    diag_vals = jnp.exp(jax.random.uniform(key_diag, (PROMPTS, HEADS, HDIM), jnp.float32, math.log(5.2), math.log(16.0)))
    off_vals = jax.random.uniform(key_off, (PROMPTS, HEADS, HDIM, HDIM), jnp.float32, -0.04, 0.04)
    off_vals = 0.5 * (off_vals + jnp.swapaxes(off_vals, -1, -2))
    eye_mat = jnp.eye(HDIM, dtype=jnp.float32)
    gram_part = off_vals * (1.0 - eye_mat) + diag_vals[..., None] * eye_mat
    cross_part = jnp.clip(1.5 * jax.random.normal(key_cross, (PROMPTS, HEADS, HDIM, HDIM), jnp.float32), -8.0, 8.0)
    return jnp.stack([gram_part, cross_part], axis=2)


def shard_levels(own_key, shape, pieces, low, high):
    factor_of, own = 1.0, jax.random.fold_in(own_key, 6)
    for dim, blocks in pieces:
        heights = jnp.exp(jax.random.uniform(jax.random.fold_in(own, dim), (blocks,), jnp.float32, low / len(pieces), high / len(pieces)))
        factor_of = factor_of * jnp.repeat(heights, shape[dim] // blocks).reshape([-1 if axis == dim else 1 for axis in range(len(shape))])
    return factor_of


def split_up(number_of, total, bound, skew):
    weights = [(1 << 20) // math.isqrt(rank ** skew) + 1 for rank in range(2, number_of + 1)]
    rest, holding = total - bound - (number_of - 1), [1] * (number_of - 1)
    while rest > 0:
        free = [i for i in range(number_of - 1) if holding[i] < bound]
        mass, budget = sum([weights[i] for i in free]), rest
        for i in free:
            more = min(bound - holding[i], max(1, budget * weights[i] // mass), rest)
            holding[i] = holding[i] + more
            rest = rest - more
    return np.array([bound] + holding)


def ragged(rng, amount, total, limit, slope):
    if amount == 2:
        one = jax.random.randint(rng, (), max(1, total - limit), min(limit, total - 1) + 1)
        return jnp.stack([one, total - one])
    lengths = jnp.asarray(split_up(amount, total, limit, slope), jnp.int32)
    couples = (amount - 1) // 2
    giver, taker = lengths[1:1 + 2 * couples:2], lengths[2:2 + 2 * couples:2]
    room = jnp.minimum(giver - 1, limit - taker)
    moved = jax.random.randint(jax.random.fold_in(rng, 1), (couples,), 0, 1 << 20) % (room + 1)
    lengths = lengths.at[1:1 + 2 * couples:2].set(giver - moved).at[2:2 + 2 * couples:2].set(taker + moved)
    return lengths[jax.random.permutation(jax.random.fold_in(rng, 2), amount)]


def noise(stream_key, shape, scale, limit, cuts=(), held_as=jnp.bfloat16):
    array = scale * jax.random.normal(stream_key, shape, jnp.float32)
    if cuts:
        array = array * shard_levels(stream_key, shape, cuts, -0.22, 0.18)
    return jnp.clip(array, -limit, limit).astype(held_as)


def setup_inputs(seed: int = 0) -> dict:
    key_of = jax.random.split(jax.random.key(seed), 16)
    tokens = noise(key_of[0], (TOKENS, D), 1.0, 6.0, ((0, 256),))
    norm_gain = jnp.clip(1.0 + 0.1 * jax.random.normal(key_of[1], (D,), jnp.float32), 0.5, 1.5)
    w_qkv = noise(key_of[2], (D, 3 * HEADS * HDIM), D ** -0.5, 0.1875)
    w_gates = noise(key_of[3], (D, 2 * HEADS), D ** -0.5, 0.1875)
    conv_weight = noise(key_of[4], (CONV, 3 * HEADS * HDIM), 0.5, 3.0, (), jnp.float32)
    conv_state = noise(key_of[5], (REQS, CONV - 1, 3 * HEADS * HDIM), 1.0, 6.0, ((0, 32),))
    decay_rate = jnp.clip(jnp.exp(jax.random.uniform(key_of[6], (HEADS,), jnp.float32, math.log(0.0005), math.log(0.1))), 0.0005, 0.1)
    ridge = jnp.clip(jnp.exp(math.log(2.0) - 2.0794415 * jax.random.uniform(key_of[7], (HEADS,), jnp.float32) ** shard_levels(key_of[7], (HEADS,), ((0, 8),), -0.2, 0.2)), 0.25, 2.0)
    w_out = noise(key_of[8], (HEADS * HDIM, D), (HEADS * HDIM) ** -0.5, 0.1875)
    cache_keys = noise(key_of[9], (POOL, PAGE, HEADS, HDIM), 0.0884, 0.59765625, ((0, 32), (2, 8)))
    cache_values = noise(key_of[10], (POOL, PAGE, HEADS, HDIM), 1.0, 6.0, ((0, 32), (2, 8)))
    page_table = draw_page_table(jax.random.fold_in(key_of[15], 71), 0)
    cache_lengths = ragged(key_of[12], REQS, REQS * PAGES_MAX * PAGE // 2, PAGES_MAX * PAGE, 2).astype(jnp.int32)
    group_prompt = draw_group_prompt(jax.random.fold_in(key_of[15], 71), 0)
    prompt_state = draw_prompt_state(jax.random.fold_in(key_of[15], 71), 0)
    return {"tokens": tokens, "norm_gain": norm_gain, "w_qkv": w_qkv, "w_gates": w_gates, "conv_weight": conv_weight, "conv_state": conv_state, "decay_rate": decay_rate, "ridge": ridge, "w_out": w_out, "cache_keys": cache_keys, "cache_values": cache_values, "page_table": page_table, "cache_lengths": cache_lengths, "group_prompt": group_prompt, "prompt_state": prompt_state}


PRECISE = lax.Precision.HIGHEST
EPS_NORM = 1e-06

def unit_rows(block):
    return block * lax.rsqrt(lax.optimization_barrier(jnp.sum(block * block, axis=-1, keepdims=True)) + EPS_NORM)

def ridge_read(query, key_rows, value_rows, write_gate, log_gamma, start_gram, start_cross, ridge_add, steps):
    length = query.shape[2]
    positions = jnp.arange(length)
    causal = positions[:, None] >= positions[None, :]
    lower_tri = causal.astype(jnp.float32)
    cumul = jnp.einsum('ts,rhs->rht', lower_tri, log_gamma, precision=PRECISE)
    spread = jnp.where(causal, cumul[..., :, None] - cumul[..., None, :], -jnp.inf)
    weights = jnp.exp(spread) * write_gate[..., None, :]
    carry_scale = jnp.exp(cumul)[..., None]
    ridge_term = ridge_add[None, :, None, None]

    def apply_op(vectors):
        from_start = jnp.einsum('rhte,rhfe->rhtf', vectors, start_gram, precision=PRECISE)
        scores = jnp.einsum('rhte,rhse->rhts', vectors, key_rows, precision=PRECISE) * weights
        return carry_scale * from_start + ridge_term * vectors + jnp.einsum('rhts,rhse->rhte', scores, key_rows, precision=PRECISE)
    solved = jnp.zeros_like(query)
    residue = query
    direction = query
    norm_now = lax.optimization_barrier(jnp.sum(residue * residue, axis=-1, keepdims=True))
    for cg_step in range(steps):
        image = apply_op(direction)
        alpha = norm_now / lax.optimization_barrier(jnp.sum(direction * image, axis=-1, keepdims=True))
        solved = solved + alpha * direction
        residue = residue - alpha * image
        norm_next = lax.optimization_barrier(jnp.sum(residue * residue, axis=-1, keepdims=True))
        direction = residue + norm_next / norm_now * direction
        norm_now = norm_next
    from_start = carry_scale * jnp.einsum('rhte,rhfe->rhtf', solved, start_cross, precision=PRECISE)
    scores = jnp.einsum('rhte,rhse->rhts', solved, key_rows, precision=PRECISE) * weights
    return from_start + jnp.einsum('rhts,rhsf->rhtf', scores, value_rows, precision=PRECISE)

def reference(tokens, norm_gain, w_qkv, w_gates, conv_weight, conv_state, decay_rate, ridge, w_out, cache_keys, cache_values, page_table, cache_lengths, group_prompt, prompt_state):
    tok_total = tokens.shape[0]
    requests = tok_total // NEW
    widened = tokens.astype(jnp.float32)
    normed = (widened * lax.rsqrt(lax.optimization_barrier(jnp.mean(widened * widened, axis=-1, keepdims=True)) + EPS_NORM) * norm_gain).astype(jnp.bfloat16)
    mixed_in = jnp.dot(normed, w_qkv, preferred_element_type=jnp.float32).astype(jnp.bfloat16)
    mixed_in = lax.optimization_barrier(mixed_in)
    gate_logits = jnp.dot(normed, w_gates, preferred_element_type=jnp.float32).reshape(tok_total, HEADS, 2)
    write_gate = jax.nn.sigmoid(gate_logits[..., 0]).astype(jnp.bfloat16)
    log_gamma = (-decay_rate * jax.nn.softplus(gate_logits[..., 1])).astype(jnp.bfloat16)
    write_gate, log_gamma = lax.optimization_barrier((write_gate, log_gamma))
    per_request = mixed_in.reshape(requests, NEW, -1)
    padded = jnp.concatenate([conv_state, per_request], axis=1).astype(jnp.float32)
    conv_sum = conv_weight[CONV - 1] * padded[:, CONV - 1:]
    for lag_step in range(1, CONV):
        conv_sum = conv_sum + conv_weight[CONV - 1 - lag_step] * padded[:, CONV - 1 - lag_step:CONV - 1 - lag_step + NEW]
    conv_sum = conv_sum.reshape(requests, NEW, HEADS, 3, HDIM)
    query = unit_rows(jax.nn.silu(conv_sum[:, :, :, 0]))
    key_vec = unit_rows(jax.nn.silu(conv_sum[:, :, :, 1]))
    value_vec = conv_sum[:, :, :, 2]
    stacked = jnp.stack([query, key_vec, value_vec], axis=3).astype(jnp.bfloat16)
    stacked = lax.optimization_barrier(stacked).astype(jnp.float32)
    stacked = jnp.transpose(stacked, (0, 2, 1, 3, 4))
    gate_pair = jnp.stack([write_gate, log_gamma], axis=-1).astype(jnp.float32).reshape(requests, NEW, HEADS, 2)
    gate_pair = jnp.transpose(gate_pair, (0, 2, 1, 3))
    token_index = jnp.arange(PAGES_MAX * PAGE)

    def one_request(pair):
        pages, length = pair
        key_pages = cache_keys[pages].reshape(PAGES_MAX * PAGE, HEADS, HDIM).astype(jnp.float32)
        value_pages = cache_values[pages].reshape(PAGES_MAX * PAGE, HEADS, HDIM).astype(jnp.float32)
        live = (token_index < length).astype(jnp.float32)[:, None, None]
        key_pages = key_pages * live
        gram = jnp.einsum('the,thf->hef', key_pages, key_pages, precision=PRECISE)
        cross = jnp.einsum('thf,the->hfe', value_pages, key_pages, precision=PRECISE)
        return jnp.stack([gram, cross], axis=1)
    cache_sums = lax.map(one_request, (page_table, cache_lengths))
    group_of = jnp.arange(requests) // REQ_GRP

    def one_read(pair):
        index, block = pair
        state = cache_sums[index] + prompt_state[group_prompt[group_of[index]]]
        gates = gate_pair[index]
        result = ridge_read(block[None, :, :, 0], block[None, :, :, 1], block[None, :, :, 2], gates[None, :, :, 0], gates[None, :, :, 1], state[None, :, 0], state[None, :, 1], ridge, CG_STEPS)
        return result[0].astype(jnp.bfloat16)
    read_out = lax.map(one_read, (jnp.arange(requests), stacked))
    read_out = jnp.transpose(read_out, (0, 2, 1, 3)).reshape(tok_total, HEADS * HDIM)
    attended = jnp.dot(read_out, w_out, preferred_element_type=jnp.float32)
    return (widened + attended).astype(jnp.bfloat16)
```

```python
import jax
import jax.numpy as jnp
from jax import lax
from jax.experimental import pallas as pl
from jax.experimental.pallas import tpu as pltpu
from jax.sharding import PartitionSpec as P

D = 1024
HEADS = 8
HDIM = 128
CONV = 4
NEW = 512
CG_STEPS = 8
PAGE = 128
POOL_DEV = 64
NY = 4
NZ = 8
TOK = NEW // HEADS
PART = 3 * HDIM
WIDE = PART + HDIM
TAIL = 16
ROWS_A = 48
ROWS_B = HDIM - ROWS_A
EPS_NORM = 1e-06
MESH = pl.DeviceIdType.MESH
F32 = jnp.float32
BF16 = jnp.bfloat16


def dot(a, b):
    return jnp.dot(a, b, preferred_element_type=F32)


def unit_rows(block):
    return block * lax.rsqrt(jnp.sum(block * block, axis=-1, keepdims=True) + EPS_NORM)


def rms_rows(block, gain):
    wide = block.astype(F32)
    mean = jnp.mean(wide * wide, axis=-1, keepdims=True)
    return (wide * lax.rsqrt(mean + EPS_NORM) * gain).astype(BF16)


def message_ids():
    ids = {}
    for dy in range(NY):
        ids["az", 1 if dy < NY // 2 else -1, 4, dy] = len(ids)
        for far in (3, 2, 1):
            for way in (1, -1):
                ids["az", way, far, dy] = len(ids)
    for dz in range(NZ):
        ids["by", 1 if dz < NZ // 2 else -1, 2, dz] = len(ids)
        for way in (1, -1):
            ids["by", way, 1, dz] = len(ids)
    for way, far in ((1, 2), (1, 1), (-1, 1)):
        ids["ay", way, far, 0] = len(ids)
    for way, far in ((1, 4), (1, 3), (1, 2), (1, 1), (-1, 3), (-1, 2), (-1, 1)):
        ids["bz", way, far, 0] = len(ids)
    return ids


IDS = message_ids()


def front_kernel(
    low_ref,
    high_ref,
    length_ref,
    prompt_of_ref,
    decay_ref,
    tokens_ref,
    gain_ref,
    gates_ref,
    conv_ref,
    stored_ref,
    prompt_ref,
    w_hbm,
    keys_hbm,
    values_hbm,
    seq_ref,
    state_ref,
    keys,
    values,
    weights,
    own_prompt,
    term_a,
    term_b,
    sum_a,
    sum_b,
    got_az,
    got_by,
    got_ay,
    got_bz,
    tail,
    normed,
    extended,
    stage,
    page_sem,
    w_sem,
    send_sem,
    recv_sem,
    head_send,
    head_recv,
):
    grp = lax.axis_index("grp")
    head = lax.axis_index("head")
    y, z = grp // NZ, grp % NZ

    def at_z(dz):
        return {"grp": y * NZ + (z + dz + NZ) % NZ}

    def at_y(dy):
        return {"grp": (y + dy + NY) % NY * NZ + z}

    def at_head(dh):
        return {"head": (head + dh) % HEADS}

    loads = []
    pieces = 4
    span = POOL_DEV // pieces
    for i in range(pieces):
        part = pl.ds(i * span, span)
        loads.append(
            pltpu.make_async_copy(keys_hbm.at[part], keys.at[part], page_sem.at[2 * i])
        )
        loads.append(
            pltpu.make_async_copy(values_hbm.at[part], values.at[part], page_sem.at[2 * i + 1])
        )
    w_loads = []
    for dh in range(HEADS):
        off = pl.multiple_of((head + dh) % HEADS * PART, HDIM)
        w_loads.append(
            pltpu.make_async_copy(w_hbm.at[:, pl.ds(off, PART)], weights.at[dh], w_sem.at[dh])
        )
    for copy in loads:
        copy.start()
    for copy in w_loads:
        copy.start()

    barrier = pltpu.get_barrier_semaphore()
    peers = [at_z(1), at_z(-1), at_y(1), at_y(-1)] + [at_head(dh) for dh in range(1, HEADS)]
    for peer in peers:
        pl.semaphore_signal(barrier, inc=1, device_id=peer, device_id_type=MESH)

    own_prompt[:, :HDIM] = prompt_ref[0, 0, 0].T
    own_prompt[:, HDIM:] = prompt_ref[0, 0, 1].T
    normed[TAIL:] = rms_rows(tokens_ref[...], gain_ref[...])

    pl.semaphore_wait(barrier, len(peers))

    sent = []

    def remote(src, dst, send, recv, peer):
        copy = pltpu.make_async_remote_copy(
            src_ref=src,
            dst_ref=dst,
            send_sem=send,
            recv_sem=recv,
            device_id=peer,
            device_id_type=MESH,
        )
        copy.start()
        sent.append(copy)
        return copy

    tail_copy = remote(
        tokens_ref.at[pl.ds(TOK - TAIL, TAIL)], tail, head_send.at[0], head_recv.at[0], at_head(1)
    )

    flying = {}
    way_slot = {1: 0, -1: 1}

    def landing(kind, way, far, piece):
        w = way_slot[way]
        return {"az": got_az, "by": got_by, "ay": got_ay, "bz": got_bz}[kind].at[w, far - 1, piece]

    def send(kind, way, far, piece, src):
        i = IDS[kind, way, far, piece]
        peer = at_z(way) if kind in ("az", "bz") else at_y(way)
        flying[kind, way, far, piece] = remote(
            src, landing(kind, way, far, piece), send_sem.at[i], recv_sem.at[i], peer
        )

    def arrived(kind, way, far, piece):
        flying[kind, way, far, piece].wait_recv()
        return landing(kind, way, far, piece)[...].astype(F32)

    for copy in loads:
        copy.wait()

    token_row = lax.broadcasted_iota(jnp.int32, (PAGE, HDIM), 0)

    def page_pair(code, length):
        count = length - (code >> 6) * PAGE
        live = (token_row < count).astype(F32).astype(BF16)
        page = code & (POOL_DEV - 1)
        own = keys[page]
        return own * live, jnp.concatenate([own, values[page]], axis=1)

    def term(dy, dz):
        request = (y + dy) % NY * NZ + (z + dz) % NZ
        length = length_ref[request]
        k0, kv0 = page_pair(low_ref[request], length)
        k1, kv1 = page_pair(high_ref[request], length)
        total = lax.dot_general(
            jnp.concatenate([k0, k1], axis=0),
            jnp.concatenate([kv0, kv1], axis=0),
            (((0,), (0,)), ((), ())),
            preferred_element_type=F32,
        )
        total = total + own_prompt[...] * (prompt_of_ref[request] == grp).astype(F32)
        total = total.astype(BF16)
        term_a[dy, dz] = total[:ROWS_A]
        term_b[dy, dz] = total[ROWS_A:]

    def send_az(far, way, dy):
        dz = far * way % NZ
        if ("az", way, far + 1, dy) in IDS:
            got = arrived("az", way, far + 1, dy)
            term_a[dy, dz] = (term_a[dy, dz].astype(F32) + got).astype(BF16)
        send("az", way, far, dy, term_a.at[dy, dz])

    def send_by(far, way, dz):
        dy = far * way % NY
        if ("by", way, far + 1, dz) in IDS:
            got = arrived("by", way, far + 1, dz)
            term_b[dy, dz] = (term_b[dy, dz].astype(F32) + got).astype(BF16)
        send("by", way, far, dz, term_b.at[dy, dz])

    def first_way(kind, far, piece):
        return 1 if (kind, 1, far, piece) in IDS else -1

    def token_start():
        tail_copy.wait_recv()
        normed[:TAIL] = rms_rows(tail[...], gain_ref[...])
        logits = lax.dot_general(
            normed[TAIL:],
            gates_ref[...],
            (((1,), (1,)), ((), ())),
            preferred_element_type=F32,
        )
        lane = lax.broadcasted_iota(jnp.int32, (TOK, 2 * HEADS), 1)
        rate = jnp.zeros((TOK, 2 * HEADS), F32)
        for h in range(HEADS):
            rate = jnp.where(lane // 2 == h, decay_ref[h], rate)
        plus = jnp.maximum(logits, 0.0) + jnp.log1p(jnp.exp(-jnp.abs(logits)))
        return jnp.where(lane % 2 == 0, jax.nn.sigmoid(logits), -rate * plus).astype(BF16)

    def head_block(dh, gates):
        which = (head + dh) % HEADS
        off = pl.multiple_of(which * PART, HDIM)
        w_loads[dh].wait()
        slot = dh % 2
        extended[slot] = dot(normed[...], weights[dh]).astype(BF16).astype(F32)

        @pl.when(head == 0)
        def _():
            extended[slot, TAIL - CONV + 1 : TAIL] = stored_ref[0, :, pl.ds(off, PART)].astype(F32)

        taps = conv_ref[:, pl.ds(off, PART)]
        mixed = taps[CONV - 1 : CONV] * extended[slot, TAIL : TAIL + TOK]
        for lag in range(1, CONV):
            rows = extended[slot, TAIL - lag : TAIL - lag + TOK]
            mixed = mixed + taps[CONV - 1 - lag : CONV - lag] * rows
        query = unit_rows(jax.nn.silu(mixed[:, :HDIM]))
        key_vec = unit_rows(jax.nn.silu(mixed[:, HDIM : 2 * HDIM]))
        row = lax.broadcasted_iota(jnp.int32, (2 * HEADS, HDIM), 0)
        col = lax.broadcasted_iota(jnp.int32, (2 * HEADS, HDIM), 1)
        pick = (row == 2 * which + (col >= HDIM // 2).astype(jnp.int32)).astype(F32).astype(BF16)
        block = jnp.concatenate(
            [query, key_vec, mixed[:, 2 * HDIM :], dot(gates, pick)], axis=1
        ).astype(BF16)
        if dh == 0:
            seq_ref[head] = block
            return None
        stage[dh] = block
        return remote(
            stage.at[dh], seq_ref.at[head], head_send.at[dh], head_recv.at[dh], at_head(dh)
        )

    for dy in (2, 0, 1, 3):
        term(dy, 4)
        send_az(4, first_way("az", 4, dy), dy)
        if dy == 2:
            send_by(2, first_way("by", 2, 4), 4)
    for dz in (3, 5, 2, 6, 1, 7, 0):
        term(2, dz)
        send_by(2, first_way("by", 2, dz), dz)
    for dz, way in ((3, 1), (5, -1)):
        for dy in (0, 1, 3):
            term(dy, dz)
    for dy in range(NY):
        send_az(3, 1, dy)
        send_az(3, -1, dy)
    for dz in (3, 5, 4):
        send_by(1, 1, dz)
        send_by(1, -1, dz)
    gates = token_start()
    head_copies = {}
    for dz in (2, 6):
        for dy in (0, 1, 3):
            term(dy, dz)
        send_by(1, 1, dz)
        send_by(1, -1, dz)
    for dh in (1, 2):
        head_copies[dh] = head_block(dh, gates)
    for dy in range(NY):
        send_az(2, 1, dy)
        send_az(2, -1, dy)
    for dz in (1, 7, 0):
        for dy in (0, 1, 3):
            term(dy, dz)
        send_by(1, 1, dz)
        send_by(1, -1, dz)
    for dh in (3, 4):
        head_copies[dh] = head_block(dh, gates)
    for dy in range(NY):
        send_az(1, 1, dy)
        send_az(1, -1, dy)
    for dh in (5, 6):
        head_copies[dh] = head_block(dh, gates)

    def send_bz(far, way):
        dz = far * way % NZ
        total = term_b[0, dz].astype(F32) + arrived("by", 1, 1, dz) + arrived("by", -1, 1, dz)
        if ("bz", way, far + 1, 0) in IDS:
            total = total + arrived("bz", way, far + 1, 0)
        sum_b[dz] = total.astype(BF16)
        send("bz", way, far, 0, sum_b.at[dz])

    def send_ay(far, way):
        dy = far * way % NY
        total = term_a[dy, 0].astype(F32) + arrived("az", 1, 1, dy) + arrived("az", -1, 1, dy)
        if ("ay", way, far + 1, 0) in IDS:
            total = total + arrived("ay", way, far + 1, 0)
        sum_a[dy] = total.astype(BF16)
        send("ay", way, far, 0, sum_a.at[dy])

    send_bz(4, 1)
    send_bz(3, -1)
    head_copies[7] = head_block(7, gates)
    send_bz(3, 1)
    send_bz(2, -1)
    head_block(0, gates)
    send_ay(2, 1)
    send_ay(1, -1)
    send_bz(2, 1)
    send_bz(1, -1)
    send_ay(1, 1)
    send_bz(1, 1)
    rows_a = term_a[0, 0].astype(F32) + arrived("az", 1, 1, 0) + arrived("az", -1, 1, 0)
    rows_a = rows_a + arrived("ay", 1, 1, 0) + arrived("ay", -1, 1, 0)
    state_ref[:ROWS_A] = rows_a
    rows_b = term_b[0, 0].astype(F32) + arrived("by", 1, 1, 0) + arrived("by", -1, 1, 0)
    rows_b = rows_b + arrived("bz", 1, 1, 0) + arrived("bz", -1, 1, 0)
    state_ref[ROWS_A:] = rows_b

    for dh in range(1, HEADS):
        source = (head + HEADS - dh) % HEADS
        pltpu.make_async_remote_copy(
            src_ref=stage.at[dh],
            dst_ref=seq_ref.at[source],
            send_sem=head_send.at[dh],
            recv_sem=head_recv.at[dh],
            device_id=at_head(dh),
            device_id_type=MESH,
        ).wait_recv()
    for copy in sent:
        copy.wait_send()


def front(low, high, lengths, prompt_of, decay, tokens, gain, gates, conv, stored, prompt, w, keys, values):
    smem = pl.BlockSpec(memory_space=pltpu.SMEM)
    vmem = pl.BlockSpec(memory_space=pltpu.VMEM)
    hbm = pl.BlockSpec(memory_space=pl.ANY)
    dma = pltpu.SemaphoreType.DMA
    return pl.pallas_call(
        front_kernel,
        name="front",
        out_shape=(
            jax.ShapeDtypeStruct((HEADS, TOK, WIDE), BF16),
            jax.ShapeDtypeStruct((HDIM, 2 * HDIM), F32),
        ),
        in_specs=[smem] * 5 + [vmem] * 6 + [hbm] * 3,
        out_specs=(vmem, vmem),
        scratch_shapes=[
            pltpu.VMEM((POOL_DEV, PAGE, HDIM), BF16),
            pltpu.VMEM((POOL_DEV, PAGE, HDIM), BF16),
            pltpu.VMEM((HEADS, D, PART), BF16),
            pltpu.VMEM((HDIM, 2 * HDIM), F32),
            pltpu.VMEM((NY, NZ, ROWS_A, 2 * HDIM), BF16),
            pltpu.VMEM((NY, NZ, ROWS_B, 2 * HDIM), BF16),
            pltpu.VMEM((NY, ROWS_A, 2 * HDIM), BF16),
            pltpu.VMEM((NZ, ROWS_B, 2 * HDIM), BF16),
            pltpu.VMEM((2, 4, NY, ROWS_A, 2 * HDIM), BF16),
            pltpu.VMEM((2, 2, NZ, ROWS_B, 2 * HDIM), BF16),
            pltpu.VMEM((2, 2, 1, ROWS_A, 2 * HDIM), BF16),
            pltpu.VMEM((2, 4, 1, ROWS_B, 2 * HDIM), BF16),
            pltpu.VMEM((TAIL, D), BF16),
            pltpu.VMEM((TAIL + TOK, D), BF16),
            pltpu.VMEM((2, TAIL + TOK, PART), F32),
            pltpu.VMEM((HEADS, TOK, WIDE), BF16),
            dma((8,)),
            dma((HEADS,)),
            dma((len(IDS),)),
            dma((len(IDS),)),
            dma((HEADS,)),
            dma((HEADS,)),
        ],
        compiler_params=pltpu.CompilerParams(
            collective_id=0, has_side_effects=True, vmem_limit_bytes=56 * 2**20
        ),
    )(low, high, lengths, prompt_of, decay, tokens, gain, gates, conv, stored, prompt, w, keys, values)


def solve_kernel(ridge_ref, seq_ref, state_ref, out_ref, keys_t, weights, start, solved, residue, direction):
    ridge = ridge_ref[0]
    gates = seq_ref[:, PART:]
    half = HDIM // 2
    lower = lax.broadcasted_iota(jnp.int32, (NEW, NEW), 0) >= lax.broadcasted_iota(
        jnp.int32, (NEW, NEW), 1
    )
    cumul = dot(lower.astype(F32).astype(BF16), gates)
    cumul_row = cumul.T[half : half + 1]
    gate_row = gates.astype(F32).T[0:1]
    cumul_col = cumul[:, half : half + 1]
    carry = jnp.exp(cumul_col)
    keys_t[...] = seq_ref[:, HDIM : 2 * HDIM].astype(F32).T.astype(BF16)
    start[...] = state_ref[...].astype(BF16)
    blocks = NEW // HDIM
    diagonal = lax.broadcasted_iota(jnp.int32, (HDIM, HDIM), 0) >= lax.broadcasted_iota(
        jnp.int32, (HDIM, HDIM), 1
    )
    for b in range(blocks):
        rows = slice(b * HDIM, (b + 1) * HDIM)
        for a in range(b + 1):
            cols = slice(a * HDIM, (a + 1) * HDIM)
            spread = cumul_col[rows] - cumul_row[:, cols]
            if a == b:
                spread = jnp.where(diagonal, spread, -jnp.inf)
            weights[rows, cols] = jnp.exp(spread) * gate_row[:, cols]
    query = seq_ref[:, :HDIM].astype(F32)
    solved[...] = jnp.zeros_like(solved)
    residue[...] = query
    direction[...] = query
    norms = tuple(
        jnp.sum(query[b * HDIM : (b + 1) * HDIM] ** 2, axis=-1, keepdims=True) for b in range(blocks)
    )

    def read(b, vectors, table, against):
        rows, seen = slice(b * HDIM, (b + 1) * HDIM), (b + 1) * HDIM
        scores = dot(vectors.astype(BF16), keys_t[:, :seen]) * weights[rows, :seen]
        opening = dot((carry[rows] * vectors).astype(BF16), table)
        return opening + dot(scores.astype(BF16), against[:seen])

    key_rows = seq_ref[:, HDIM : 2 * HDIM]

    def step(_, norms):
        following = []
        for b in range(blocks):
            rows = slice(b * HDIM, (b + 1) * HDIM)
            ahead = direction[rows]
            image = read(b, ahead, start[:, :HDIM], key_rows) + ridge * ahead
            alpha = norms[b] / jnp.sum(ahead * image, axis=-1, keepdims=True)
            solved[rows] = solved[rows] + alpha * ahead
            left = residue[rows] - alpha * image
            norm = jnp.sum(left * left, axis=-1, keepdims=True)
            residue[rows] = left
            direction[rows] = left + norm / norms[b] * ahead
            following.append(norm)
        return tuple(following)

    lax.fori_loop(0, CG_STEPS, step, norms)
    for b in range(blocks):
        rows = slice(b * HDIM, (b + 1) * HDIM)
        result = read(b, solved[rows], start[:, HDIM:], seq_ref[:, 2 * HDIM : PART])
        out_ref[rows] = result.astype(BF16)


def solve(ridge, seq, state):
    smem = pl.BlockSpec(memory_space=pltpu.SMEM)
    vmem = pl.BlockSpec(memory_space=pltpu.VMEM)
    return pl.pallas_call(
        solve_kernel,
        name="solve",
        out_shape=jax.ShapeDtypeStruct((NEW, HDIM), BF16),
        in_specs=[smem, vmem, vmem],
        out_specs=vmem,
        scratch_shapes=[
            pltpu.VMEM((HDIM, NEW), BF16),
            pltpu.VMEM((NEW, NEW), F32),
            pltpu.VMEM((HDIM, 2 * HDIM), BF16),
            pltpu.VMEM((NEW, HDIM), F32),
            pltpu.VMEM((NEW, HDIM), F32),
            pltpu.VMEM((NEW, HDIM), F32),
        ],
        compiler_params=pltpu.CompilerParams(vmem_limit_bytes=32 * 2**20),
    )(ridge, seq, state)


def back_kernel(read_ref, tokens_ref, w_hbm, out_ref, weights, got, w_sem, send_sem, recv_sem):
    head = lax.axis_index("head")
    load = pltpu.make_async_copy(w_hbm, weights, w_sem)
    load.start()
    barrier = pltpu.get_barrier_semaphore()
    for dh in range(1, HEADS):
        pl.semaphore_signal(
            barrier, inc=1, device_id={"head": (head + dh) % HEADS}, device_id_type=MESH
        )
    pl.semaphore_wait(barrier, HEADS - 1)
    copies = []
    for dh in range(1, HEADS):
        peer = (head + dh) % HEADS
        copy = pltpu.make_async_remote_copy(
            src_ref=read_ref.at[peer],
            dst_ref=got.at[head],
            send_sem=send_sem.at[dh],
            recv_sem=recv_sem.at[dh],
            device_id={"head": peer},
            device_id_type=MESH,
        )
        copy.start()
        copies.append(copy)
    got[head] = read_ref[head]
    load.wait()
    for dh in range(1, HEADS):
        source = (head + HEADS - dh) % HEADS
        pltpu.make_async_remote_copy(
            src_ref=read_ref.at[source],
            dst_ref=got.at[source],
            send_sem=send_sem.at[dh],
            recv_sem=recv_sem.at[dh],
            device_id={"head": source},
            device_id_type=MESH,
        ).wait_recv()
    rows = jnp.concatenate([got[h] for h in range(HEADS)], axis=1)
    out_ref[...] = (tokens_ref[...].astype(F32) + dot(rows, weights[...])).astype(BF16)
    for copy in copies:
        copy.wait_send()


def back(read_out, tokens, w_out):
    vmem = pl.BlockSpec(memory_space=pltpu.VMEM)
    return pl.pallas_call(
        back_kernel,
        name="back",
        out_shape=jax.ShapeDtypeStruct((TOK, D), BF16),
        in_specs=[vmem, vmem, pl.BlockSpec(memory_space=pl.ANY)],
        out_specs=vmem,
        scratch_shapes=[
            pltpu.VMEM((HEADS * HDIM, D), BF16),
            pltpu.VMEM((HEADS, TOK, HDIM), BF16),
            pltpu.SemaphoreType.DMA,
            pltpu.SemaphoreType.DMA((HEADS,)),
            pltpu.SemaphoreType.DMA((HEADS,)),
        ],
        compiler_params=pltpu.CompilerParams(
            collective_id=1, has_side_effects=True, vmem_limit_bytes=32 * 2**20
        ),
    )(read_out, tokens, w_out)


def shards(
    tokens,
    norm_gain,
    w_qkv,
    w_gates,
    conv_weight,
    conv_state,
    decay_rate,
    ridge,
    w_out,
    cache_keys,
    cache_values,
    page_table,
    cache_lengths,
    group_prompt,
    prompt_state,
):
    local = page_table - lax.axis_index("grp") * POOL_DEV
    here = (local >= 0) & (local < POOL_DEV)
    code = jnp.arange(page_table.shape[1])[None, :] * POOL_DEV + local
    low = jnp.min(jnp.where(here, code, 1 << 20), axis=1)
    high = jnp.max(jnp.where(here, code, -1), axis=1)
    seq, state = front(
        low,
        high,
        cache_lengths,
        group_prompt,
        decay_rate,
        tokens,
        norm_gain.reshape(1, D),
        w_gates.T,
        conv_weight,
        conv_state,
        prompt_state,
        w_qkv,
        cache_keys.reshape(POOL_DEV, PAGE, HDIM),
        cache_values.reshape(POOL_DEV, PAGE, HDIM),
    )
    read_out = solve(ridge, seq.reshape(NEW, WIDE), state)
    return back(read_out.reshape(HEADS, TOK, HDIM), tokens, w_out)


def solution(mesh):
    placed = (
        P(("grp", "head"), None),
        P(),
        P(),
        P(),
        P(),
        P("grp", None, None),
        P(),
        P("head"),
        P(),
        P("grp", None, "head", None),
        P("grp", None, "head", None),
        P(),
        P(),
        P(),
        P("grp", "head", None, None, None),
    )
    return jax.shard_map(
        shards, mesh=mesh, in_specs=placed, out_specs=P(("grp", "head"), None), check_vma=False
    )
```

```python
import jax
import jax.numpy as jnp
from jax import lax
from jax.experimental import pallas as pl
from jax.experimental.pallas import tpu as pltpu
from jax.sharding import PartitionSpec as P

D = 1024
HEADS = 8
HDIM = 128
CONV = 4
NEW = 512
CG_STEPS = 8
PAGE = 128
POOL_DEV = 64
NY = 4
NZ = 8
TOK = NEW // HEADS
PART = 3 * HDIM
WIDE = PART + HDIM
TAIL = 16
ROWS_A = 48
ROWS_B = HDIM - ROWS_A
EPS_NORM = 1e-06
MESH = pl.DeviceIdType.MESH
F32 = jnp.float32
BF16 = jnp.bfloat16


def dot(a, b):
    return jnp.dot(a, b, preferred_element_type=F32)


def unit_rows(block):
    return block * lax.rsqrt(jnp.sum(block * block, axis=-1, keepdims=True) + EPS_NORM)


def rms_rows(block, gain):
    wide = block.astype(F32)
    mean = jnp.mean(wide * wide, axis=-1, keepdims=True)
    return (wide * lax.rsqrt(mean + EPS_NORM) * gain).astype(BF16)


def task_table():
    tasks = {}

    def add(name, cost, after=(), waits=(), link=None, size=0):
        tasks[name] = (cost, tuple(after), tuple(waits), link, size)

    size_a, size_b = ROWS_A * 4 * HDIM, ROWS_B * 4 * HDIM
    for dy in range(NY):
        for dz in range(NZ):
            add(("term", dy, dz), 0.1)
    for dy in range(NY):
        for way in (1, -1):
            for far in (4, 3, 2, 1):
                if far == 4 and (way == 1) != (dy < NY // 2):
                    continue
                before = [("az", way, far + 1, dy)]
                before = [m for m in before if m in tasks]
                add(("az", way, far, dy), 0.03, [("term", dy, far * way % NZ)], before, ("z", way), size_a)
    for dz in range(NZ):
        for way in (1, -1):
            for far in (2, 1):
                if far == 2 and (way == 1) != (dz < NZ // 2):
                    continue
                before = [("by", way, far + 1, dz)]
                before = [m for m in before if m in tasks]
                add(("by", way, far, dz), 0.03, [("term", far * way % NY, dz)], before, ("y", way), size_b)
    for way, far in ((1, 2), (1, 1), (-1, 1)):
        dy = far * way % NY
        before = [("az", 1, 1, dy), ("az", -1, 1, dy)]
        before += [m for m in [("ay", way, far + 1, 0)] if m in tasks]
        add(("ay", way, far, 0), 0.03, [("term", dy, 0)], before, ("y", way), size_a)
    for way, far in ((1, 4), (1, 3), (1, 2), (1, 1), (-1, 3), (-1, 2), (-1, 1)):
        dz = far * way % NZ
        before = [("by", 1, 1, dz), ("by", -1, 1, dz)]
        before += [m for m in [("bz", way, far + 1, 0)] if m in tasks]
        add(("bz", way, far, 0), 0.03, [("term", 0, dz)], before, ("z", way), size_b)
    add(("tokens",), 0.35)
    for i in range(HEADS):
        dh = (i + 1) % HEADS
        add(("head", dh), 0.33, [("tokens",)], (), ("x", dh) if dh else None, 40000)
    add(("ready", 0), 0.5, [("head", 0)], [("head", dh) for dh in range(1, HEADS)])
    for b in range(NEW // HDIM):
        add(("ready", b + 1), 0.2, [("ready", 0)])
    last = [("az", way, 1, 0) for way in (1, -1)] + [("ay", way, 1, 0) for way in (1, -1)]
    last += [("by", way, 1, 0) for way in (1, -1)] + [("bz", way, 1, 0) for way in (1, -1)]
    add(("end",), 0.05, [("term", 0, 0)] + [("ready", b) for b in range(NEW // HDIM + 1)], last)
    return tasks


def task_order(tasks, hop=1.7, rate=46500.0, backlog=0.9):
    longest = {}
    for name in reversed(list(tasks)):
        longest[name] = tasks[name][0]
    for _ in range(12):
        for name, (cost, after, waits, _, _) in tasks.items():
            for m in after:
                longest[m] = max(longest[m], tasks[m][0] + longest[name])
            for m in waits:
                flight = hop + tasks[m][4] / rate
                longest[m] = max(longest[m], tasks[m][0] + flight + longest[name])
    now, order, landed, free = 0.0, [], {}, {}
    left = dict(tasks)
    while left:
        best, soonest = None, 1e9
        for name, (cost, after, waits, link, size) in left.items():
            if any(m in left for m in after) or any(m not in landed for m in waits):
                continue
            ready = max([landed[m] for m in waits] + [free.get(link, 0.0) - backlog])
            if ready > now:
                soonest = min(soonest, ready)
            elif best is None or longest[name] > longest[best]:
                best = name
        if best is None:
            now = soonest
            continue
        cost, _, _, link, size = left.pop(best)
        order.append(best)
        now += cost
        if link is not None:
            free[link] = max(now, free.get(link, 0.0)) + size / rate
            landed[best] = free[link] + hop
    return order


TASKS = task_table()
ORDER = task_order(TASKS)
IDS = {}
for task in TASKS:
    if task[0] in ("az", "by", "ay", "bz"):
        IDS[task] = len(IDS)


def layer_kernel(
    low_ref,
    high_ref,
    length_ref,
    prompt_of_ref,
    decay_ref,
    ridge_ref,
    tokens_ref,
    gain_ref,
    gates_ref,
    conv_ref,
    stored_ref,
    prompt_ref,
    w_hbm,
    keys_hbm,
    values_hbm,
    out_hbm,
    out_ref,
    seq_ref,
    start,
    keys,
    values,
    weights,
    own_prompt,
    term_a,
    term_b,
    sum_a,
    sum_b,
    got_az,
    got_by,
    got_ay,
    got_bz,
    tail,
    normed,
    extended,
    stage,
    page_sem,
    w_sem,
    send_sem,
    recv_sem,
    head_send,
    head_recv,
    keys_t,
    scales,
    rows_ref,
    carry,
    solved,
    residue,
    direction,
    out_w,
    read_rows,
    got,
    out_sem,
    back_send,
    back_recv,
):
    grp = lax.axis_index("grp")
    head = lax.axis_index("head")
    y, z = grp // NZ, grp % NZ

    def at_z(dz):
        return {"grp": y * NZ + (z + dz + NZ) % NZ}

    def at_y(dy):
        return {"grp": (y + dy + NY) % NY * NZ + z}

    def at_head(dh):
        return {"head": (head + dh) % HEADS}

    loads = []
    pieces = 4
    span = POOL_DEV // pieces
    for i in range(pieces):
        part = pl.ds(i * span, span)
        loads.append(
            pltpu.make_async_copy(keys_hbm.at[part], keys.at[part], page_sem.at[2 * i])
        )
        loads.append(
            pltpu.make_async_copy(values_hbm.at[part], values.at[part], page_sem.at[2 * i + 1])
        )
    w_loads = []
    for dh in range(HEADS):
        off = pl.multiple_of((head + dh) % HEADS * PART, HDIM)
        w_loads.append(
            pltpu.make_async_copy(w_hbm.at[:, pl.ds(off, PART)], weights.at[dh], w_sem.at[dh])
        )
    for copy in loads:
        copy.start()
    for copy in w_loads:
        copy.start()
    out_load = pltpu.make_async_copy(out_hbm, out_w, out_sem)
    out_load.start()

    barrier = pltpu.get_barrier_semaphore()
    peers = [at_z(1), at_z(-1), at_y(1), at_y(-1)] + [at_head(dh) for dh in range(1, HEADS)]
    for peer in peers:
        pl.semaphore_signal(barrier, inc=1, device_id=peer, device_id_type=MESH)

    own_prompt[:, :HDIM] = prompt_ref[0, 0, 0].T
    own_prompt[:, HDIM:] = prompt_ref[0, 0, 1].T
    normed[TAIL:] = rms_rows(tokens_ref[...], gain_ref[...])

    pl.semaphore_wait(barrier, len(peers))

    sent = []

    def remote(src, dst, send, recv, peer):
        copy = pltpu.make_async_remote_copy(
            src_ref=src,
            dst_ref=dst,
            send_sem=send,
            recv_sem=recv,
            device_id=peer,
            device_id_type=MESH,
        )
        copy.start()
        sent.append(copy)
        return copy

    tail_copy = remote(
        tokens_ref.at[pl.ds(TOK - TAIL, TAIL)], tail, head_send.at[0], head_recv.at[0], at_head(1)
    )

    flying = {}
    way_slot = {1: 0, -1: 1}

    def landing(kind, way, far, piece):
        w = way_slot[way]
        return {"az": got_az, "by": got_by, "ay": got_ay, "bz": got_bz}[kind].at[w, far - 1, piece]

    def send(kind, way, far, piece, src):
        i = IDS[kind, way, far, piece]
        peer = at_z(way) if kind in ("az", "bz") else at_y(way)
        flying[kind, way, far, piece] = remote(
            src, landing(kind, way, far, piece), send_sem.at[i], recv_sem.at[i], peer
        )

    def arrived(kind, way, far, piece):
        flying[kind, way, far, piece].wait_recv()
        return landing(kind, way, far, piece)[...].astype(F32)

    for copy in loads:
        copy.wait()

    token_row = lax.broadcasted_iota(jnp.int32, (PAGE, HDIM), 0)

    def page_pair(code, length):
        count = length - (code >> 6) * PAGE
        live = (token_row < count).astype(F32).astype(BF16)
        page = code & (POOL_DEV - 1)
        own = keys[page]
        return own * live, jnp.concatenate([own, values[page]], axis=1)

    def term(dy, dz):
        request = (y + dy) % NY * NZ + (z + dz) % NZ
        length = length_ref[request]
        k0, kv0 = page_pair(low_ref[request], length)
        k1, kv1 = page_pair(high_ref[request], length)
        total = lax.dot_general(
            jnp.concatenate([k0, k1], axis=0),
            jnp.concatenate([kv0, kv1], axis=0),
            (((0,), (0,)), ((), ())),
            preferred_element_type=F32,
        )
        total = total + own_prompt[...] * (prompt_of_ref[request] == grp).astype(F32)
        total = total.astype(BF16)
        term_a[dy, dz] = total[:ROWS_A]
        term_b[dy, dz] = total[ROWS_A:]

    def send_az(far, way, dy):
        dz = far * way % NZ
        if ("az", way, far + 1, dy) in IDS:
            got = arrived("az", way, far + 1, dy)
            term_a[dy, dz] = (term_a[dy, dz].astype(F32) + got).astype(BF16)
        send("az", way, far, dy, term_a.at[dy, dz])

    def send_by(far, way, dz):
        dy = far * way % NY
        if ("by", way, far + 1, dz) in IDS:
            got = arrived("by", way, far + 1, dz)
            term_b[dy, dz] = (term_b[dy, dz].astype(F32) + got).astype(BF16)
        send("by", way, far, dz, term_b.at[dy, dz])

    def first_way(kind, far, piece):
        return 1 if (kind, 1, far, piece) in IDS else -1

    def token_start():
        tail_copy.wait_recv()
        normed[:TAIL] = rms_rows(tail[...], gain_ref[...])
        logits = lax.dot_general(
            normed[TAIL:],
            gates_ref[...],
            (((1,), (1,)), ((), ())),
            preferred_element_type=F32,
        )
        lane = lax.broadcasted_iota(jnp.int32, (TOK, 2 * HEADS), 1)
        rate = jnp.zeros((TOK, 2 * HEADS), F32)
        for h in range(HEADS):
            rate = jnp.where(lane // 2 == h, decay_ref[h], rate)
        plus = jnp.maximum(logits, 0.0) + jnp.log1p(jnp.exp(-jnp.abs(logits)))
        return jnp.where(lane % 2 == 0, jax.nn.sigmoid(logits), -rate * plus).astype(BF16)

    def head_block(dh, gates):
        which = (head + dh) % HEADS
        off = pl.multiple_of(which * PART, HDIM)
        w_loads[dh].wait()
        slot = dh % 2
        extended[slot] = dot(normed[...], weights[dh]).astype(BF16).astype(F32)

        @pl.when(head == 0)
        def _():
            extended[slot, TAIL - CONV + 1 : TAIL] = stored_ref[0, :, pl.ds(off, PART)].astype(F32)

        taps = conv_ref[:, pl.ds(off, PART)]
        mixed = taps[CONV - 1 : CONV] * extended[slot, TAIL : TAIL + TOK]
        for lag in range(1, CONV):
            rows = extended[slot, TAIL - lag : TAIL - lag + TOK]
            mixed = mixed + taps[CONV - 1 - lag : CONV - lag] * rows
        query = unit_rows(jax.nn.silu(mixed[:, :HDIM]))
        key_vec = unit_rows(jax.nn.silu(mixed[:, HDIM : 2 * HDIM]))
        row = lax.broadcasted_iota(jnp.int32, (2 * HEADS, HDIM), 0)
        col = lax.broadcasted_iota(jnp.int32, (2 * HEADS, HDIM), 1)
        pick = (row == 2 * which + (col >= HDIM // 2).astype(jnp.int32)).astype(F32).astype(BF16)
        block = jnp.concatenate(
            [query, key_vec, mixed[:, 2 * HDIM :], dot(gates, pick)], axis=1
        ).astype(BF16)
        if dh == 0:
            seq_ref[head] = block
            return None
        stage[dh] = block
        return remote(
            stage.at[dh], seq_ref.at[head], head_send.at[dh], head_recv.at[dh], at_head(dh)
        )

    def send_bz(far, way):
        dz = far * way % NZ
        total = term_b[0, dz].astype(F32) + arrived("by", 1, 1, dz) + arrived("by", -1, 1, dz)
        if ("bz", way, far + 1, 0) in IDS:
            total = total + arrived("bz", way, far + 1, 0)
        sum_b[dz] = total.astype(BF16)
        send("bz", way, far, 0, sum_b.at[dz])

    def send_ay(far, way):
        dy = far * way % NY
        total = term_a[dy, 0].astype(F32) + arrived("az", 1, 1, dy) + arrived("az", -1, 1, dy)
        if ("ay", way, far + 1, 0) in IDS:
            total = total + arrived("ay", way, far + 1, 0)
        sum_a[dy] = total.astype(BF16)
        send("ay", way, far, 0, sum_a.at[dy])

    def all_heads():
        for dh in range(1, HEADS):
            source = (head + HEADS - dh) % HEADS
            pltpu.make_async_remote_copy(
                src_ref=stage.at[dh],
                dst_ref=seq_ref.at[source],
                send_sem=head_send.at[dh],
                recv_sem=head_recv.at[dh],
                device_id=at_head(dh),
                device_id_type=MESH,
            ).wait_recv()

    blocks = NEW // HDIM

    def part_of(first):
        return seq_ref[:, :, first : first + HDIM].reshape(NEW, HDIM)

    def prepare():
        all_heads()
        gates = part_of(PART)
        half = HDIM // 2
        row = lax.broadcasted_iota(jnp.int32, (HDIM, HDIM), 0)
        spread_out = dot(gates, (row == half).astype(F32).astype(BF16)).astype(BF16)
        lower = lax.broadcasted_iota(jnp.int32, (NEW, NEW), 0) >= lax.broadcasted_iota(
            jnp.int32, (NEW, NEW), 1
        )
        cumul = dot(lower.astype(F32).astype(BF16), spread_out)
        carry[...] = cumul
        rows_ref[0:1] = cumul.T[0:1]
        rows_ref[1:2] = gates.astype(F32).T[0:1]
        keys_t[...] = part_of(HDIM).astype(F32).T.astype(BF16)
        query = part_of(0).astype(F32)
        solved[...] = jnp.zeros_like(solved)
        residue[...] = query
        direction[...] = query

    def scale_rows(b):
        rows = slice(b * HDIM, (b + 1) * HDIM)
        for a in range(b + 1):
            cols = slice(a * HDIM, (a + 1) * HDIM)
            spread = carry[rows] - rows_ref[0:1, cols]
            if a == b:
                causal = lax.broadcasted_iota(
                    jnp.int32, (HDIM, HDIM), 0
                ) >= lax.broadcasted_iota(jnp.int32, (HDIM, HDIM), 1)
                spread = jnp.where(causal, spread, -jnp.inf)
            scales[rows, cols] = jnp.exp(spread) * rows_ref[1:2, cols]
        carry[rows] = jnp.exp(carry[rows])

    def close():
        rows_a = term_a[0, 0].astype(F32) + arrived("az", 1, 1, 0) + arrived("az", -1, 1, 0)
        rows_a = rows_a + arrived("ay", 1, 1, 0) + arrived("ay", -1, 1, 0)
        start[:ROWS_A] = rows_a.astype(BF16)
        rows_b = term_b[0, 0].astype(F32) + arrived("by", 1, 1, 0) + arrived("by", -1, 1, 0)
        rows_b = rows_b + arrived("bz", 1, 1, 0) + arrived("bz", -1, 1, 0)
        start[ROWS_A:] = rows_b.astype(BF16)

    gates = None
    for task in ORDER:
        kind = task[0]
        if kind == "term":
            term(task[1], task[2])
        elif kind == "az":
            send_az(task[2], task[1], task[3])
        elif kind == "by":
            send_by(task[2], task[1], task[3])
        elif kind == "ay":
            send_ay(task[2], task[1])
        elif kind == "bz":
            send_bz(task[2], task[1])
        elif kind == "tokens":
            gates = token_start()
        elif kind == "head":
            head_block(task[1], gates)
        elif kind == "ready":
            prepare() if task[1] == 0 else scale_rows(task[1] - 1)
        else:
            close()

    ridge = ridge_ref[0]

    def read(b, vectors, table, against):
        rows, seen = slice(b * HDIM, (b + 1) * HDIM), (b + 1) * HDIM
        scores = dot(vectors.astype(BF16), keys_t[:, :seen]) * scales[rows, :seen]
        opening = dot((carry[rows] * vectors).astype(BF16), table)
        return opening + dot(scores.astype(BF16), against[:seen])

    key_rows = part_of(HDIM)

    def step(_, norms):
        following = []
        for b in range(blocks):
            rows = slice(b * HDIM, (b + 1) * HDIM)
            ahead = direction[rows]
            image = read(b, ahead, start[:, :HDIM], key_rows) + ridge * ahead
            alpha = norms[b] / jnp.sum(ahead * image, axis=-1, keepdims=True)
            solved[rows] = solved[rows] + alpha * ahead
            left = residue[rows] - alpha * image
            norm = jnp.sum(left * left, axis=-1, keepdims=True)
            residue[rows] = left
            direction[rows] = left + norm / norms[b] * ahead
            following.append(norm)
        return tuple(following)

    norms = []
    for b in range(blocks):
        query = residue[b * HDIM : (b + 1) * HDIM]
        norms.append(jnp.sum(query * query, axis=-1, keepdims=True))
    lax.fori_loop(0, CG_STEPS, step, tuple(norms))
    for b in range(blocks):
        rows = slice(b * HDIM, (b + 1) * HDIM)
        result = read(b, solved[rows], start[:, HDIM:], part_of(2 * HDIM)).astype(BF16)
        read_rows[2 * b] = result[:TOK]
        read_rows[2 * b + 1] = result[TOK:]
    for dh in range(1, HEADS):
        peer = (head + dh) % HEADS
        remote(read_rows.at[peer], got.at[head], back_send.at[dh], back_recv.at[dh], at_head(dh))
    got[head] = read_rows[head]
    out_load.wait()
    total = tokens_ref[...].astype(F32)
    chip, core = head // 2, head % 2
    for dx in (0, 1, 3, 2):
        there = (chip + dx) % 4
        for c in range(2):
            source = there * 2 + c

            @pl.when(source != head)
            def _():
                pltpu.make_async_remote_copy(
                    src_ref=read_rows.at[source],
                    dst_ref=got.at[source],
                    send_sem=back_send.at[(head + HEADS - source) % HEADS],
                    recv_sem=back_recv.at[(head + HEADS - source) % HEADS],
                    device_id={"head": source},
                    device_id_type=MESH,
                ).wait_recv()

        rows = jnp.concatenate([got[there * 2], got[there * 2 + 1]], axis=1)
        depth = pl.multiple_of(there * 2 * HDIM, 2 * HDIM)
        total = total + dot(rows, out_w[pl.ds(depth, 2 * HDIM)])
    out_ref[...] = total.astype(BF16)
    for copy in sent:
        copy.wait_send()


def layer(*operands):
    smem = pl.BlockSpec(memory_space=pltpu.SMEM)
    vmem = pl.BlockSpec(memory_space=pltpu.VMEM)
    hbm = pl.BlockSpec(memory_space=pl.ANY)
    dma = pltpu.SemaphoreType.DMA
    return pl.pallas_call(
        layer_kernel,
        name="layer",
        out_shape=jax.ShapeDtypeStruct((TOK, D), BF16),
        in_specs=[smem] * 6 + [vmem] * 6 + [hbm] * 4,
        out_specs=vmem,
        scratch_shapes=[
            pltpu.VMEM((HEADS, TOK, WIDE), BF16),
            pltpu.VMEM((HDIM, 2 * HDIM), BF16),
            pltpu.VMEM((POOL_DEV, PAGE, HDIM), BF16),
            pltpu.VMEM((POOL_DEV, PAGE, HDIM), BF16),
            pltpu.VMEM((HEADS, D, PART), BF16),
            pltpu.VMEM((HDIM, 2 * HDIM), F32),
            pltpu.VMEM((NY, NZ, ROWS_A, 2 * HDIM), BF16),
            pltpu.VMEM((NY, NZ, ROWS_B, 2 * HDIM), BF16),
            pltpu.VMEM((NY, ROWS_A, 2 * HDIM), BF16),
            pltpu.VMEM((NZ, ROWS_B, 2 * HDIM), BF16),
            pltpu.VMEM((2, 4, NY, ROWS_A, 2 * HDIM), BF16),
            pltpu.VMEM((2, 2, NZ, ROWS_B, 2 * HDIM), BF16),
            pltpu.VMEM((2, 2, 1, ROWS_A, 2 * HDIM), BF16),
            pltpu.VMEM((2, 4, 1, ROWS_B, 2 * HDIM), BF16),
            pltpu.VMEM((TAIL, D), BF16),
            pltpu.VMEM((TAIL + TOK, D), BF16),
            pltpu.VMEM((2, TAIL + TOK, PART), F32),
            pltpu.VMEM((HEADS, TOK, WIDE), BF16),
            dma((8,)),
            dma((HEADS,)),
            dma((len(IDS),)),
            dma((len(IDS),)),
            dma((HEADS,)),
            dma((HEADS,)),
            pltpu.VMEM((HDIM, NEW), BF16),
            pltpu.VMEM((NEW, NEW), F32),
            pltpu.VMEM((8, NEW), F32),
            pltpu.VMEM((NEW, HDIM), F32),
            pltpu.VMEM((NEW, HDIM), F32),
            pltpu.VMEM((NEW, HDIM), F32),
            pltpu.VMEM((NEW, HDIM), F32),
            pltpu.VMEM((HEADS * HDIM, D), BF16),
            pltpu.VMEM((HEADS, TOK, HDIM), BF16),
            pltpu.VMEM((HEADS, TOK, HDIM), BF16),
            dma,
            dma((HEADS,)),
            dma((HEADS,)),
        ],
        compiler_params=pltpu.CompilerParams(
            collective_id=0, has_side_effects=True, vmem_limit_bytes=60 * 2**20
        ),
    )(*operands)


def shards(
    tokens,
    norm_gain,
    w_qkv,
    w_gates,
    conv_weight,
    conv_state,
    decay_rate,
    ridge,
    w_out,
    cache_keys,
    cache_values,
    page_table,
    cache_lengths,
    group_prompt,
    prompt_state,
):
    local = page_table - lax.axis_index("grp") * POOL_DEV
    here = (local >= 0) & (local < POOL_DEV)
    code = jnp.arange(page_table.shape[1])[None, :] * POOL_DEV + local
    low = jnp.min(jnp.where(here, code, 1 << 20), axis=1)
    high = jnp.max(jnp.where(here, code, -1), axis=1)
    return layer(
        low,
        high,
        cache_lengths,
        group_prompt,
        decay_rate,
        ridge,
        tokens,
        norm_gain.reshape(1, D),
        w_gates.T,
        conv_weight,
        conv_state,
        prompt_state,
        w_qkv,
        cache_keys.reshape(POOL_DEV, PAGE, HDIM),
        cache_values.reshape(POOL_DEV, PAGE, HDIM),
        w_out,
    )


def solution(mesh):
    placed = (
        P(("grp", "head"), None),
        P(),
        P(),
        P(),
        P(),
        P("grp", None, None),
        P(),
        P("head"),
        P(),
        P("grp", None, "head", None),
        P("grp", None, "head", None),
        P(),
        P(),
        P(),
        P("grp", "head", None, None, None),
    )
    return jax.shard_map(
        shards, mesh=mesh, in_specs=placed, out_specs=P(("grp", "head"), None), check_vma=False
    )
```

```python
import jax
import jax.numpy as jnp
from jax import lax
from jax.experimental import pallas as pl
from jax.experimental.pallas import tpu as pltpu
from jax.sharding import PartitionSpec as P

D = 1024
HEADS = 8
HDIM = 128
CONV = 4
NEW = 512
CG_STEPS = 8
PAGE = 128
POOL_DEV = 64
REQS = 32
NY = 4
NZ = 8
TOK = NEW // HEADS
PART = 3 * HDIM
WIDE = PART + HDIM
TAIL = 16
ROWS_A = 48
ROWS_B = HDIM - ROWS_A
EPS_NORM = 1e-06
MESH = pl.DeviceIdType.MESH
F32 = jnp.float32
BF16 = jnp.bfloat16


def dot(a, b):
    return jnp.dot(a, b, preferred_element_type=F32)


def unit_rows(block):
    return block * lax.rsqrt(jnp.sum(block * block, axis=-1, keepdims=True) + EPS_NORM)


def rms_rows(block, gain):
    wide = block.astype(F32)
    mean = jnp.mean(wide * wide, axis=-1, keepdims=True)
    return (wide * lax.rsqrt(mean + EPS_NORM) * gain).astype(BF16)


def task_table():
    tasks = {}

    def add(name, cost, after=(), waits=(), link=None, size=0):
        tasks[name] = (cost, tuple(after), tuple(waits), link, size)

    size_a, size_b = ROWS_A * 4 * HDIM, ROWS_B * 4 * HDIM
    for dy in range(NY):
        for dz in range(NZ):
            add(("term", dy, dz), 0.1)
    for dy in range(NY):
        for way in (1, -1):
            for far in (4, 3, 2, 1):
                if far == 4 and (way == 1) != (dy < NY // 2):
                    continue
                before = [("az", way, far + 1, dy)]
                before = [m for m in before if m in tasks]
                add(("az", way, far, dy), 0.03, [("term", dy, far * way % NZ)], before, ("z", way), size_a)
    for dz in range(NZ):
        for way in (1, -1):
            for far in (2, 1):
                if far == 2 and (way == 1) != (dz < NZ // 2):
                    continue
                before = [("by", way, far + 1, dz)]
                before = [m for m in before if m in tasks]
                add(("by", way, far, dz), 0.03, [("term", far * way % NY, dz)], before, ("y", way), size_b)
    for way, far in ((1, 2), (1, 1), (-1, 1)):
        dy = far * way % NY
        before = [("az", 1, 1, dy), ("az", -1, 1, dy)]
        before += [m for m in [("ay", way, far + 1, 0)] if m in tasks]
        add(("ay", way, far, 0), 0.03, [("term", dy, 0)], before, ("y", way), size_a)
    for way, far in ((1, 4), (1, 3), (1, 2), (1, 1), (-1, 3), (-1, 2), (-1, 1)):
        dz = far * way % NZ
        before = [("by", 1, 1, dz), ("by", -1, 1, dz)]
        before += [m for m in [("bz", way, far + 1, 0)] if m in tasks]
        add(("bz", way, far, 0), 0.03, [("term", 0, dz)], before, ("z", way), size_b)
    add(("tokens",), 0.35)
    for i in range(HEADS):
        dh = (i + 1) % HEADS
        add(("head", dh), 0.33, [("tokens",)], (), ("x", dh) if dh else None, 40000)
    add(("ready", 0), 0.5, [("head", 0)], [("head", dh) for dh in range(1, HEADS)])
    for b in range(NEW // HDIM):
        add(("ready", b + 1), 0.2, [("ready", 0)])
    last = [("az", way, 1, 0) for way in (1, -1)] + [("ay", way, 1, 0) for way in (1, -1)]
    last += [("by", way, 1, 0) for way in (1, -1)] + [("bz", way, 1, 0) for way in (1, -1)]
    add(("end",), 0.05, [("term", 0, 0)] + [("ready", b) for b in range(NEW // HDIM + 1)], last)
    return tasks


def task_order(tasks, hop=1.7, rate=46500.0, backlog=0.9):
    longest = {}
    for name in reversed(list(tasks)):
        longest[name] = tasks[name][0]
    for _ in range(12):
        for name, (cost, after, waits, _, _) in tasks.items():
            for m in after:
                longest[m] = max(longest[m], tasks[m][0] + longest[name])
            for m in waits:
                flight = hop + tasks[m][4] / rate
                longest[m] = max(longest[m], tasks[m][0] + flight + longest[name])
    now, order, landed, free = 0.0, [], {}, {}
    left = dict(tasks)
    while left:
        best, soonest = None, 1e9
        for name, (cost, after, waits, link, size) in left.items():
            if any(m in left for m in after) or any(m not in landed for m in waits):
                continue
            ready = max([landed[m] for m in waits] + [free.get(link, 0.0) - backlog])
            if ready > now:
                soonest = min(soonest, ready)
            elif best is None or longest[name] > longest[best]:
                best = name
        if best is None:
            now = soonest
            continue
        cost, _, _, link, size = left.pop(best)
        order.append(best)
        now += cost
        if link is not None:
            free[link] = max(now, free.get(link, 0.0)) + size / rate
            landed[best] = free[link] + hop
    return order


TASKS = task_table()
ORDER = task_order(TASKS)
IDS = {}
for task in TASKS:
    if task[0] in ("az", "by", "ay", "bz"):
        IDS[task] = len(IDS)


def layer_kernel(
    length_ref,
    prompt_of_ref,
    decay_ref,
    ridge_ref,
    tokens_ref,
    gain_ref,
    gates_ref,
    conv_ref,
    stored_ref,
    prompt_ref,
    table_ref,
    w_hbm,
    keys_hbm,
    values_hbm,
    out_hbm,
    out_ref,
    seq_ref,
    start,
    keys,
    values,
    weights,
    own_prompt,
    term_a,
    term_b,
    sum_a,
    sum_b,
    got_az,
    got_by,
    got_ay,
    got_bz,
    tail,
    normed,
    extended,
    stage,
    page_sem,
    w_sem,
    send_sem,
    recv_sem,
    head_send,
    head_recv,
    keys_t,
    scales,
    rows_ref,
    carry,
    solved,
    residue,
    direction,
    out_w,
    read_rows,
    got,
    out_sem,
    back_send,
    back_recv,
    code_rows,
    codes,
    code_sem,
):
    grp = lax.axis_index("grp")
    head = lax.axis_index("head")
    y, z = grp // NZ, grp % NZ

    def at_z(dz):
        return {"grp": y * NZ + (z + dz + NZ) % NZ}

    def at_y(dy):
        return {"grp": (y + dy + NY) % NY * NZ + z}

    def at_head(dh):
        return {"head": (head + dh) % HEADS}

    local = table_ref[...] - grp * POOL_DEV
    here = (local >= 0) & (local < POOL_DEV)
    code = lax.broadcasted_iota(jnp.int32, local.shape, 1) * POOL_DEV + local
    low = jnp.min(jnp.where(here, code, 1 << 20), axis=1, keepdims=True)
    high = jnp.max(jnp.where(here, code, -1), axis=1, keepdims=True)
    side = lax.broadcasted_iota(jnp.int32, code_rows.shape, 1)
    code_rows[...] = jnp.where(side == 0, low, high)
    code_load = pltpu.make_async_copy(code_rows, codes, code_sem)

    loads = []
    pieces = 4
    span = POOL_DEV // pieces
    for i in range(pieces):
        part = pl.ds(i * span, span)
        loads.append(
            pltpu.make_async_copy(keys_hbm.at[part], keys.at[part], page_sem.at[2 * i])
        )
        loads.append(
            pltpu.make_async_copy(values_hbm.at[part], values.at[part], page_sem.at[2 * i + 1])
        )
    w_loads = []
    for dh in range(HEADS):
        off = pl.multiple_of((head + dh) % HEADS * PART, HDIM)
        w_loads.append(
            pltpu.make_async_copy(w_hbm.at[:, pl.ds(off, PART)], weights.at[dh], w_sem.at[dh])
        )
    for copy in loads:
        copy.start()
    for copy in w_loads:
        copy.start()
    out_load = pltpu.make_async_copy(out_hbm, out_w, out_sem)
    out_load.start()

    barrier = pltpu.get_barrier_semaphore()
    peers = [at_z(1), at_z(-1), at_y(1), at_y(-1)] + [at_head(dh) for dh in range(1, HEADS)]
    for peer in peers:
        pl.semaphore_signal(barrier, inc=1, device_id=peer, device_id_type=MESH)

    code_load.start()
    own_prompt[:, :HDIM] = prompt_ref[0, 0, 0].T
    own_prompt[:, HDIM:] = prompt_ref[0, 0, 1].T
    normed[TAIL:] = rms_rows(tokens_ref[...], gain_ref[...])

    pl.semaphore_wait(barrier, len(peers))

    sent = []

    def remote(src, dst, send, recv, peer):
        copy = pltpu.make_async_remote_copy(
            src_ref=src,
            dst_ref=dst,
            send_sem=send,
            recv_sem=recv,
            device_id=peer,
            device_id_type=MESH,
        )
        copy.start()
        sent.append(copy)
        return copy

    tail_copy = remote(
        tokens_ref.at[pl.ds(TOK - TAIL, TAIL)], tail, head_send.at[0], head_recv.at[0], at_head(1)
    )

    flying = {}
    way_slot = {1: 0, -1: 1}

    def landing(kind, way, far, piece):
        w = way_slot[way]
        return {"az": got_az, "by": got_by, "ay": got_ay, "bz": got_bz}[kind].at[w, far - 1, piece]

    def send(kind, way, far, piece, src):
        i = IDS[kind, way, far, piece]
        peer = at_z(way) if kind in ("az", "bz") else at_y(way)
        flying[kind, way, far, piece] = remote(
            src, landing(kind, way, far, piece), send_sem.at[i], recv_sem.at[i], peer
        )

    def arrived(kind, way, far, piece):
        flying[kind, way, far, piece].wait_recv()
        return landing(kind, way, far, piece)[...].astype(F32)

    code_load.wait()
    for copy in loads:
        copy.wait()

    token_row = lax.broadcasted_iota(jnp.int32, (PAGE, HDIM), 0)

    def page_pair(code, length):
        count = length - (code >> 6) * PAGE
        live = (token_row < count).astype(F32).astype(BF16)
        page = code & (POOL_DEV - 1)
        own = keys[page]
        return own * live, jnp.concatenate([own, values[page]], axis=1)

    def term(dy, dz):
        request = (y + dy) % NY * NZ + (z + dz) % NZ
        length = length_ref[request]
        k0, kv0 = page_pair(codes[request, 0], length)
        k1, kv1 = page_pair(codes[request, 1], length)
        total = lax.dot_general(
            jnp.concatenate([k0, k1], axis=0),
            jnp.concatenate([kv0, kv1], axis=0),
            (((0,), (0,)), ((), ())),
            preferred_element_type=F32,
        )
        total = total + own_prompt[...] * (prompt_of_ref[request] == grp).astype(F32)
        total = total.astype(BF16)
        term_a[dy, dz] = total[:ROWS_A]
        term_b[dy, dz] = total[ROWS_A:]

    def send_az(far, way, dy):
        dz = far * way % NZ
        if ("az", way, far + 1, dy) in IDS:
            got = arrived("az", way, far + 1, dy)
            term_a[dy, dz] = (term_a[dy, dz].astype(F32) + got).astype(BF16)
        send("az", way, far, dy, term_a.at[dy, dz])

    def send_by(far, way, dz):
        dy = far * way % NY
        if ("by", way, far + 1, dz) in IDS:
            got = arrived("by", way, far + 1, dz)
            term_b[dy, dz] = (term_b[dy, dz].astype(F32) + got).astype(BF16)
        send("by", way, far, dz, term_b.at[dy, dz])

    def first_way(kind, far, piece):
        return 1 if (kind, 1, far, piece) in IDS else -1

    def token_start():
        tail_copy.wait_recv()
        normed[:TAIL] = rms_rows(tail[...], gain_ref[...])
        logits = lax.dot_general(
            normed[TAIL:],
            gates_ref[...],
            (((1,), (1,)), ((), ())),
            preferred_element_type=F32,
        )
        lane = lax.broadcasted_iota(jnp.int32, (TOK, 2 * HEADS), 1)
        rate = jnp.zeros((TOK, 2 * HEADS), F32)
        for h in range(HEADS):
            rate = jnp.where(lane // 2 == h, decay_ref[h], rate)
        plus = jnp.maximum(logits, 0.0) + jnp.log1p(jnp.exp(-jnp.abs(logits)))
        return jnp.where(lane % 2 == 0, jax.nn.sigmoid(logits), -rate * plus).astype(BF16)

    def head_block(dh, gates):
        which = (head + dh) % HEADS
        off = pl.multiple_of(which * PART, HDIM)
        w_loads[dh].wait()
        slot = dh % 2
        extended[slot] = dot(normed[...], weights[dh]).astype(BF16).astype(F32)

        @pl.when(head == 0)
        def _():
            extended[slot, TAIL - CONV + 1 : TAIL] = stored_ref[0, :, pl.ds(off, PART)].astype(F32)

        taps = conv_ref[:, pl.ds(off, PART)]
        mixed = taps[CONV - 1 : CONV] * extended[slot, TAIL : TAIL + TOK]
        for lag in range(1, CONV):
            rows = extended[slot, TAIL - lag : TAIL - lag + TOK]
            mixed = mixed + taps[CONV - 1 - lag : CONV - lag] * rows
        query = unit_rows(jax.nn.silu(mixed[:, :HDIM]))
        key_vec = unit_rows(jax.nn.silu(mixed[:, HDIM : 2 * HDIM]))
        row = lax.broadcasted_iota(jnp.int32, (2 * HEADS, HDIM), 0)
        col = lax.broadcasted_iota(jnp.int32, (2 * HEADS, HDIM), 1)
        pick = (row == 2 * which + (col >= HDIM // 2).astype(jnp.int32)).astype(F32).astype(BF16)
        block = jnp.concatenate(
            [query, key_vec, mixed[:, 2 * HDIM :], dot(gates, pick)], axis=1
        ).astype(BF16)
        if dh == 0:
            seq_ref[head] = block
            return None
        stage[dh] = block
        return remote(
            stage.at[dh], seq_ref.at[head], head_send.at[dh], head_recv.at[dh], at_head(dh)
        )

    def send_bz(far, way):
        dz = far * way % NZ
        total = term_b[0, dz].astype(F32) + arrived("by", 1, 1, dz) + arrived("by", -1, 1, dz)
        if ("bz", way, far + 1, 0) in IDS:
            total = total + arrived("bz", way, far + 1, 0)
        sum_b[dz] = total.astype(BF16)
        send("bz", way, far, 0, sum_b.at[dz])

    def send_ay(far, way):
        dy = far * way % NY
        total = term_a[dy, 0].astype(F32) + arrived("az", 1, 1, dy) + arrived("az", -1, 1, dy)
        if ("ay", way, far + 1, 0) in IDS:
            total = total + arrived("ay", way, far + 1, 0)
        sum_a[dy] = total.astype(BF16)
        send("ay", way, far, 0, sum_a.at[dy])

    def all_heads():
        for dh in range(1, HEADS):
            source = (head + HEADS - dh) % HEADS
            pltpu.make_async_remote_copy(
                src_ref=stage.at[dh],
                dst_ref=seq_ref.at[source],
                send_sem=head_send.at[dh],
                recv_sem=head_recv.at[dh],
                device_id=at_head(dh),
                device_id_type=MESH,
            ).wait_recv()

    blocks = NEW // HDIM

    def part_of(first):
        return seq_ref[:, :, first : first + HDIM].reshape(NEW, HDIM)

    def prepare():
        all_heads()
        gates = part_of(PART)
        half = HDIM // 2
        row = lax.broadcasted_iota(jnp.int32, (HDIM, HDIM), 0)
        spread_out = dot(gates, (row == half).astype(F32).astype(BF16)).astype(BF16)
        lower = lax.broadcasted_iota(jnp.int32, (NEW, NEW), 0) >= lax.broadcasted_iota(
            jnp.int32, (NEW, NEW), 1
        )
        cumul = dot(lower.astype(F32).astype(BF16), spread_out)
        carry[...] = cumul
        rows_ref[0:1] = cumul.T[0:1]
        rows_ref[1:2] = gates.astype(F32).T[0:1]
        keys_t[...] = part_of(HDIM).astype(F32).T.astype(BF16)
        query = part_of(0).astype(F32)
        solved[...] = jnp.zeros_like(solved)
        residue[...] = query
        direction[...] = query

    def scale_rows(b):
        rows = slice(b * HDIM, (b + 1) * HDIM)
        for a in range(b + 1):
            cols = slice(a * HDIM, (a + 1) * HDIM)
            spread = carry[rows] - rows_ref[0:1, cols]
            if a == b:
                causal = lax.broadcasted_iota(
                    jnp.int32, (HDIM, HDIM), 0
                ) >= lax.broadcasted_iota(jnp.int32, (HDIM, HDIM), 1)
                spread = jnp.where(causal, spread, -jnp.inf)
            scales[rows, cols] = jnp.exp(spread) * rows_ref[1:2, cols]
        carry[rows] = jnp.exp(carry[rows])

    def close():
        rows_a = term_a[0, 0].astype(F32) + arrived("az", 1, 1, 0) + arrived("az", -1, 1, 0)
        rows_a = rows_a + arrived("ay", 1, 1, 0) + arrived("ay", -1, 1, 0)
        start[:ROWS_A] = rows_a.astype(BF16)
        rows_b = term_b[0, 0].astype(F32) + arrived("by", 1, 1, 0) + arrived("by", -1, 1, 0)
        rows_b = rows_b + arrived("bz", 1, 1, 0) + arrived("bz", -1, 1, 0)
        start[ROWS_A:] = rows_b.astype(BF16)

    gates = None
    for task in ORDER:
        kind = task[0]
        if kind == "term":
            term(task[1], task[2])
        elif kind == "az":
            send_az(task[2], task[1], task[3])
        elif kind == "by":
            send_by(task[2], task[1], task[3])
        elif kind == "ay":
            send_ay(task[2], task[1])
        elif kind == "bz":
            send_bz(task[2], task[1])
        elif kind == "tokens":
            gates = token_start()
        elif kind == "head":
            head_block(task[1], gates)
        elif kind == "ready":
            prepare() if task[1] == 0 else scale_rows(task[1] - 1)
        else:
            close()

    ridge = ridge_ref[0]

    def read(b, vectors, table, against):
        rows, seen = slice(b * HDIM, (b + 1) * HDIM), (b + 1) * HDIM
        scores = dot(vectors.astype(BF16), keys_t[:, :seen]) * scales[rows, :seen]
        opening = dot((carry[rows] * vectors).astype(BF16), table)
        return opening + dot(scores.astype(BF16), against[:seen])

    key_rows = part_of(HDIM)

    def step(_, norms):
        following = []
        for b in range(blocks):
            rows = slice(b * HDIM, (b + 1) * HDIM)
            ahead = direction[rows]
            image = read(b, ahead, start[:, :HDIM], key_rows) + ridge * ahead
            alpha = norms[b] / jnp.sum(ahead * image, axis=-1, keepdims=True)
            solved[rows] = solved[rows] + alpha * ahead
            left = residue[rows] - alpha * image
            norm = jnp.sum(left * left, axis=-1, keepdims=True)
            residue[rows] = left
            direction[rows] = left + norm / norms[b] * ahead
            following.append(norm)
        return tuple(following)

    norms = []
    for b in range(blocks):
        query = residue[b * HDIM : (b + 1) * HDIM]
        norms.append(jnp.sum(query * query, axis=-1, keepdims=True))
    lax.fori_loop(0, CG_STEPS, step, tuple(norms), unroll=True)
    for b in range(blocks):
        rows = slice(b * HDIM, (b + 1) * HDIM)
        result = read(b, solved[rows], start[:, HDIM:], part_of(2 * HDIM)).astype(BF16)
        read_rows[2 * b] = result[:TOK]
        read_rows[2 * b + 1] = result[TOK:]
    for dh in range(1, HEADS):
        peer = (head + dh) % HEADS
        remote(read_rows.at[peer], got.at[head], back_send.at[dh], back_recv.at[dh], at_head(dh))
    got[head] = read_rows[head]
    out_load.wait()
    total = tokens_ref[...].astype(F32)
    chip, core = head // 2, head % 2
    for dx in (0, 1, 3, 2):
        there = (chip + dx) % 4
        for c in range(2):
            source = there * 2 + c

            @pl.when(source != head)
            def _():
                pltpu.make_async_remote_copy(
                    src_ref=read_rows.at[source],
                    dst_ref=got.at[source],
                    send_sem=back_send.at[(head + HEADS - source) % HEADS],
                    recv_sem=back_recv.at[(head + HEADS - source) % HEADS],
                    device_id={"head": source},
                    device_id_type=MESH,
                ).wait_recv()

        rows = jnp.concatenate([got[there * 2], got[there * 2 + 1]], axis=1)
        depth = pl.multiple_of(there * 2 * HDIM, 2 * HDIM)
        total = total + dot(rows, out_w[pl.ds(depth, 2 * HDIM)])
    out_ref[...] = total.astype(BF16)
    for copy in sent:
        copy.wait_send()


def layer(*operands):
    smem = pl.BlockSpec(memory_space=pltpu.SMEM)
    vmem = pl.BlockSpec(memory_space=pltpu.VMEM)
    hbm = pl.BlockSpec(memory_space=pl.ANY)
    dma = pltpu.SemaphoreType.DMA
    return pl.pallas_call(
        layer_kernel,
        name="layer",
        out_shape=jax.ShapeDtypeStruct((TOK, D), BF16),
        in_specs=[smem] * 4 + [vmem] * 7 + [hbm] * 4,
        out_specs=vmem,
        scratch_shapes=[
            pltpu.VMEM((HEADS, TOK, WIDE), BF16),
            pltpu.VMEM((HDIM, 2 * HDIM), BF16),
            pltpu.VMEM((POOL_DEV, PAGE, HDIM), BF16),
            pltpu.VMEM((POOL_DEV, PAGE, HDIM), BF16),
            pltpu.VMEM((HEADS, D, PART), BF16),
            pltpu.VMEM((HDIM, 2 * HDIM), F32),
            pltpu.VMEM((NY, NZ, ROWS_A, 2 * HDIM), BF16),
            pltpu.VMEM((NY, NZ, ROWS_B, 2 * HDIM), BF16),
            pltpu.VMEM((NY, ROWS_A, 2 * HDIM), BF16),
            pltpu.VMEM((NZ, ROWS_B, 2 * HDIM), BF16),
            pltpu.VMEM((2, 4, NY, ROWS_A, 2 * HDIM), BF16),
            pltpu.VMEM((2, 2, NZ, ROWS_B, 2 * HDIM), BF16),
            pltpu.VMEM((2, 2, 1, ROWS_A, 2 * HDIM), BF16),
            pltpu.VMEM((2, 4, 1, ROWS_B, 2 * HDIM), BF16),
            pltpu.VMEM((TAIL, D), BF16),
            pltpu.VMEM((TAIL + TOK, D), BF16),
            pltpu.VMEM((2, TAIL + TOK, PART), F32),
            pltpu.VMEM((HEADS, TOK, WIDE), BF16),
            dma((8,)),
            dma((HEADS,)),
            dma((len(IDS),)),
            dma((len(IDS),)),
            dma((HEADS,)),
            dma((HEADS,)),
            pltpu.VMEM((HDIM, NEW), BF16),
            pltpu.VMEM((NEW, NEW), F32),
            pltpu.VMEM((8, NEW), F32),
            pltpu.VMEM((NEW, HDIM), F32),
            pltpu.VMEM((NEW, HDIM), F32),
            pltpu.VMEM((NEW, HDIM), F32),
            pltpu.VMEM((NEW, HDIM), F32),
            pltpu.VMEM((HEADS * HDIM, D), BF16),
            pltpu.VMEM((HEADS, TOK, HDIM), BF16),
            pltpu.VMEM((HEADS, TOK, HDIM), BF16),
            dma,
            dma((HEADS,)),
            dma((HEADS,)),
            pltpu.VMEM((REQS, HDIM), jnp.int32),
            pltpu.SMEM((REQS, HDIM), jnp.int32),
            dma,
        ],
        compiler_params=pltpu.CompilerParams(
            collective_id=0, has_side_effects=True, vmem_limit_bytes=60 * 2**20
        ),
    )(*operands)


def shards(
    tokens,
    norm_gain,
    w_qkv,
    w_gates,
    conv_weight,
    conv_state,
    decay_rate,
    ridge,
    w_out,
    cache_keys,
    cache_values,
    page_table,
    cache_lengths,
    group_prompt,
    prompt_state,
):
    return layer(
        cache_lengths,
        group_prompt,
        decay_rate,
        ridge,
        tokens,
        norm_gain.reshape(1, D),
        w_gates.T,
        conv_weight,
        conv_state,
        prompt_state,
        page_table,
        w_qkv,
        cache_keys.reshape(POOL_DEV, PAGE, HDIM),
        cache_values.reshape(POOL_DEV, PAGE, HDIM),
        w_out,
    )


def solution(mesh):
    placed = (
        P(("grp", "head"), None),
        P(),
        P(),
        P(),
        P(),
        P("grp", None, None),
        P(),
        P("head"),
        P(),
        P("grp", None, "head", None),
        P("grp", None, "head", None),
        P(),
        P(),
        P(),
        P("grp", "head", None, None, None),
    )
    return jax.shard_map(
        shards, mesh=mesh, in_specs=placed, out_specs=P(("grp", "head"), None), check_vma=False
    )
```
